32 devices in a mesh: gx: 16 (over z, x, core), gy: 2 (over y).
Axes of the slice: x: 2, y: 2, z: 4, core: 2. Of those that a mesh axis runs over, the one named last changes fastest.
Arguments:
- adjoint: bfloat16 [256, 256, 512], P('gx', 'gy'), may hold values from -6 to 6
- conduct_x: float32 [256, 256], P('gx', 'gy'), may hold values from 0.02 to 0.24
- conduct_y: float32 [256, 256], P('gx', 'gy'), may hold values from 0.02 to 0.24
- pick_weights: bfloat16 [64, 256, 256], P(None, 'gx', 'gy'), may hold values from -0.03125 to 0.03125
- owner_order: int32 [64], replicated, may hold values from 0 to 63, each once
Outputs:
- smoothed: bfloat16 [256, 256, 512], P('gx', 'gy')
- representer: float32 [64, 512], P(('gx', 'gy'))
The draws below stay inside these ranges and needn't reach their ends.
Inputs may be any that keep to these rules, and one draw needn't show every extreme that they name: `owner_order`: each of 0 to 63 appears once.
All inputs are finite; a program needn't handle non-finite values.
Results may differ from the reference program's by a relative error of at most 0.0029.
Values may be sent and summed in bfloat16 or wider, within the bound.
A program may use at most 64 MiB of HBM per device.

```python
import math
import jax
import jax.numpy as jnp

PANEL = 256
PANELS = 2
STEPS = 4
COLUMNS = 512
PICKS = 64
NX = 256
NY = 256


def raised(entries, stream_key, source, target, shards_of, factor):
    owner, partner = [(jnp.arange(entries.shape[axis_at]) // (entries.shape[axis_at] // shards_of)).reshape([-1 if axis == axis_at else 1 for axis in range(entries.ndim)]) for axis_at in (source, target)]
    chosen = jax.random.permutation(stream_key, shards_of)[partner]
    strong = (owner == chosen) | (owner == (partner + shards_of // 2) % shards_of)
    return jnp.where(strong, factor * entries, entries)


def shard_levels(stream_key, dims, shards, smallest, largest):
    level = 1.0
    for axis_at, shards_of in shards:
        steps = jax.random.uniform(jax.random.fold_in(jax.random.fold_in(stream_key, 6), axis_at), (shards_of,), jnp.float32, smallest / len(shards), largest / len(shards))
        level = level * jnp.repeat(jnp.exp(steps), dims[axis_at] // shards_of).reshape((-1,) + (1,) * (len(dims) - 1 - axis_at))
    return level


def normal_values(stream_key, extent, deviation, reach, split=(), kind=jnp.bfloat16):
    values = deviation * jax.random.normal(stream_key, extent, jnp.float32)
    if split:
        values = values * shard_levels(stream_key, extent, split, -0.22, 0.18)
    return jnp.clip(values, -reach, reach).astype(kind)


def bell_draw_with(rng, extent, deviation, reach, split, heavy, kind=jnp.bfloat16):
    drawn = deviation * jax.random.normal(rng, extent, jnp.float32)
    if split:
        drawn = drawn * shard_levels(rng, extent, split, -0.22, 0.18)
    return jnp.clip(raised(drawn, jax.random.fold_in(rng, 3), *heavy), -reach, reach).astype(kind)


def setup_inputs(seed: int = 0) -> dict:
    splits = jax.random.split(jax.random.key(seed), 6)
    return {
        "adjoint": normal_values(splits[0], (NX, NY, COLUMNS), 1.0, 6.0, ((0, 16), (1, 2))),
        "conduct_x": jnp.clip(jnp.exp(math.log(0.24) - 2.4849066 * jax.random.uniform(splits[1], (NX, NY), jnp.float32) ** shard_levels(splits[1], (NX, NY), ((0, 16), (1, 2)), -0.2, 0.2)), 0.02, 0.24),
        "conduct_y": jnp.clip(jnp.exp(math.log(0.24) - 2.4849066 * jax.random.uniform(splits[2], (NX, NY), jnp.float32) ** shard_levels(splits[2], (NX, NY), ((0, 16), (1, 2)), -0.2, 0.2)), 0.02, 0.24),
        "pick_weights": bell_draw_with(splits[3], (PICKS, NX, NY), (NX * NY) ** -0.5, 0.03125, ((1, 16), (2, 2)), (1, 0, 16, 2.0)),
        "owner_order": jax.random.permutation(splits[4], PICKS).astype(jnp.int32),
    }


def diffuse(field, conx, cony):
    centre = field[1:-1, 1:-1]
    above = field[:-2, 1:-1]
    below = field[2:, 1:-1]
    leftside = field[1:-1, :-2]
    rightside = field[1:-1, 2:]
    result = centre + conx[:-2, 1:-1, None] * (above - centre)
    result = result + conx[1:-1, 1:-1, None] * (below - centre)
    result = result + cony[1:-1, :-2, None] * (leftside - centre)
    result = result + cony[1:-1, 1:-1, None] * (rightside - centre)
    return result


def reference(adjoint, conduct_x, conduct_y, pick_weights, owner_order):
    rows_idx = jnp.arange(NX, dtype=jnp.int32)[:, None]
    cols_idx = jnp.arange(NY, dtype=jnp.int32)[None, :]
    conx = jnp.where(rows_idx < NX - 1, conduct_x, jnp.float32(0.0))
    cony = jnp.where(cols_idx < NY - 1, conduct_y, jnp.float32(0.0))
    conx_pad = jnp.pad(conx, 1)
    cony_pad = jnp.pad(cony, 1)
    flat_weights = pick_weights.reshape(PICKS, NX * NY)
    smooth_list = []
    repr_list = []
    for panel in range(PANELS):
        field = adjoint[:, :, panel * PANEL:(panel + 1) * PANEL].astype(jnp.float32)
        for step in range(STEPS):
            field = diffuse(jnp.pad(field, ((1, 1), (1, 1), (0, 0))), conx_pad, cony_pad)
        rounded = field.astype(jnp.bfloat16)
        smooth_list.append(rounded)
        partial_value = jnp.dot(flat_weights, rounded.reshape(NX * NY, PANEL), preferred_element_type=jnp.float32)
        repr_list.append(jnp.take(partial_value, owner_order, axis=0))
    return jnp.concatenate(smooth_list, axis=2), jnp.concatenate(repr_list, axis=1)
```

```python
import functools

import jax
import jax.numpy as jnp
from jax import lax
from jax.experimental import pallas as pl
from jax.experimental.pallas import tpu as pltpu
from jax.sharding import PartitionSpec as P

STEPS = 4
LANES = 128
SUB = 8
MESH = pl.DeviceIdType.MESH
DIRS = ((0, 1), (0, -1), (1, 1), (1, -1), (-1, 1), (-1, -1), (1, 0), (-1, 0))
F32 = jnp.float32
BF16 = jnp.bfloat16


def dir_id(dx, dy):
    return DIRS.index((dx, dy))


def kernel(
    nx, ny, adj, kx_ref, ky_ref, w_ref, order_ref, out, rep,
    eb, yb, kn, kxb, kyb, u, w32, wt, ps, rbuf,
    load_sem, a_send, a_recv, k_send, k_recv, r_send, r_recv,
):
    cx, cy, cols = adj.shape
    groups = cols // LANES
    ex = cx + 2 * STEPS
    ey = cy + SUB
    picks = w_ref.shape[0]
    n = nx * ny
    tile = ps.shape[0] // n
    gx = lax.axis_index("gx")
    gy = lax.axis_index("gy")
    me = gx * ny + gy

    def dev(t):
        return (t // ny, lax.rem(t, ny))

    barrier = pltpu.get_barrier_semaphore()

    @pl.loop(1, n)
    def _(k):
        pl.semaphore_signal(
            barrier, inc=1, device_id=dev(lax.rem(me + k, n)), device_id_type=MESH
        )

    own = pltpu.make_async_copy(adj, eb.at[pl.ds(STEPS, cx)], load_sem)
    own.start()

    def present(dx, dy):
        ok = None
        for d, g, size in ((dx, gx, nx), (dy, gy, ny)):
            if d == 1:
                c = g < size - 1
            elif d == -1:
                c = g > 0
            else:
                continue
            ok = c if ok is None else jnp.logical_and(ok, c)
        return ok

    def region(sx, sy):
        rows = {-1: pl.ds(0, STEPS), 0: pl.ds(STEPS, cx), 1: pl.ds(STEPS + cx, STEPS)}[sx]
        if sy == 0:
            return eb.at[rows]
        return yb.at[0 if sy == 1 else 1, rows]

    def copies(dx, dy):
        sx, sy = -dx, -dy
        slot, mine = dir_id(sx, sy), dir_id(dx, dy)
        target = (gx + dx, gy + dy)
        src = adj
        if dx:
            src = src.at[pl.ds(cx - STEPS if dx == 1 else 0, STEPS)]
        if dy:
            src = src.at[:, pl.ds(cy - SUB if dy == 1 else 0, SUB)]
        dst = region(sx, sy)
        result = []
        for a, kref in enumerate((kx_ref, ky_ref)):
            result.append(
                pltpu.make_async_remote_copy(
                    src_ref=kref, dst_ref=kn.at[slot, a], send_sem=k_send.at[mine, a],
                    recv_sem=k_recv.at[slot, a], device_id=target, device_id_type=MESH,
                )
            )
        parts = [(src, dst)]
        if dy == 0:
            parts = [
                (src.at[:, :, pl.ds(q * LANES, LANES)], dst.at[:, :, pl.ds(q * LANES, LANES)])
                for q in range(groups)
            ]
        for q, (s, d) in enumerate(parts):
            result.append(
                pltpu.make_async_remote_copy(
                    src_ref=s, dst_ref=d, send_sem=a_send.at[mine, q],
                    recv_sem=a_recv.at[slot, q], device_id=target, device_id_type=MESH,
                )
            )
        return result

    pick_ids = lax.broadcasted_iota(jnp.int32, (picks, picks), 0)
    chosen = jnp.where(pick_ids == order_ref[...], F32(1), F32(0)).astype(BF16)
    w32[...] = w_ref[...].astype(F32).reshape(picks * cx, LANES)

    def sort_weights():
        for x in range(cx):
            row = w32[pl.ds(x, picks, stride=cx), :].astype(BF16)
            row = lax.dot_general(
                chosen, row, (((0,), (0,)), ((), ())), preferred_element_type=F32
            )
            wt[:, x * LANES : (x + 1) * LANES] = row.astype(BF16)

    pl.semaphore_wait(barrier, n - 1)

    for dx, dy in DIRS:
        @pl.when(present(dx, dy))
        def _(dx=dx, dy=dy):
            for c in copies(dx, dy):
                c.start()

        @pl.when(jnp.logical_not(present(dx, dy)))
        def _(dx=dx, dy=dy):
            part = region(dx, dy)
            part[...] = jnp.zeros(part.shape, BF16)
            kn[dir_id(dx, dy)] = jnp.zeros(kn.shape[1:], F32)

    sort_weights()

    def wait_recv(dx, dy, what):
        @pl.when(present(dx, dy))
        def _():
            slot = dir_id(dx, dy)
            if what == "k":
                for a in range(2):
                    pltpu.make_async_copy(kn.at[slot, a], kn.at[slot, a], k_recv.at[slot, a]).wait()
            elif what == "a":
                part = region(dx, dy)
                pltpu.make_async_copy(part, part, a_recv.at[slot, 0]).wait()
            else:
                part = region(dx, dy).at[:, :, pl.ds(what * LANES, LANES)]
                pltpu.make_async_copy(part, part, a_recv.at[slot, what]).wait()

    for d in DIRS:
        wait_recv(*d, "k")

    low = lax.broadcasted_iota(jnp.int32, (SUB, cx), 0) < STEPS
    place = lax.broadcasted_iota(jnp.int32, (ey, cx), 0)
    for a, (kref, store) in enumerate(((kx_ref, kxb), (ky_ref, kyb))):
        for sx in (-1, 0, 1):
            def block(sy):
                if sx == 0 and sy == 0:
                    return kref[...]
                return kn[dir_id(sx, sy), a]

            main = block(0).T
            tail = jnp.where(low, block(1).T[:SUB], block(-1).T[cy - SUB :])
            whole = jnp.concatenate([main, tail], axis=0)
            if a == 1:
                whole = jnp.where(
                    jnp.logical_and(place == cy - 1, gy == ny - 1), F32(0), whole
                )
            rows = {-1: range(cx - STEPS, cx), 0: range(cx), 1: range(STEPS)}[sx]
            base = {-1: 0, 0: STEPS, 1: STEPS + cx}[sx]
            for i, r in enumerate(rows):
                column = jnp.broadcast_to(whole[:, r : r + 1], (ey, LANES))
                if a == 0 and sx == 0 and r == cx - 1:
                    column = jnp.where(gx == nx - 1, F32(0), column)
                store[base + i] = column

    low_lane = lax.broadcasted_iota(jnp.int32, (SUB, LANES), 0) < STEPS

    def lanes(q):
        if isinstance(q, int):
            return pl.ds(q * LANES, LANES)
        return pl.ds(pl.multiple_of(q * LANES, LANES), LANES)

    def assemble(q, lo, hi):
        @pl.loop(lo, hi)
        def _(e):
            u[0, q, e, :cy] = eb[e, :, lanes(q)].astype(F32)
            right = yb[0, e, :, lanes(q)].astype(F32)
            left = yb[1, e, :, lanes(q)].astype(F32)
            u[0, q, e, cy:] = jnp.where(low_lane, right, left)

    def sweep(level, q, lo, hi):
        here = u[level, q, lo]
        before = kxb[lo - 1] * (here - u[level, q, lo - 1])

        def body(e, carry):
            here, before = carry
            below = u[level, q, e + 1]
            after = kxb[e] * (below - here)
            side = kyb[e] * (pltpu.roll(here, ey - 1, 0) - here)
            value = (here + (after - before)) + (side - pltpu.roll(side, 1, 0))
            if level < STEPS - 1:
                u[level + 1, q, e] = value
            else:
                out[e - STEPS, :, lanes(q)] = value[:cy].astype(BF16)
            return below, after

        lax.fori_loop(lo, hi, body, (here, before))

    def product(lo, hi):
        return jnp.dot(
            wt[:, lo * LANES : hi * LANES],
            out[lo:hi].reshape((hi - lo) * cy, cols),
            preferred_element_type=F32,
        )

    own.wait()
    for d in DIRS[:2]:
        wait_recv(*d, "a")

    @pl.loop(0, groups)
    def _(q):
        assemble(q, STEPS, STEPS + cx)
        for s in range(1, STEPS + 1):
            sweep(s - 1, q, STEPS + s, STEPS + cx - s)

    for d in DIRS[2:6]:
        wait_recv(*d, "a")
    for q in range(groups):
        for d in DIRS[6:]:
            wait_recv(*d, q)
        assemble(q, 0, STEPS)
        assemble(q, STEPS + cx, ex)
        for s in range(1, STEPS + 1):
            sweep(s - 1, q, s, STEPS + s)
            sweep(s - 1, q, STEPS + cx - s, ex - s)

    total = product(0, cx)
    for q in range(groups):
        ps[pl.ds(q, picks, stride=groups), :] = total[:, q * LANES : (q + 1) * LANES]

    def reduce_copy(k):
        t = lax.rem(me + k, n)
        return pltpu.make_async_remote_copy(
            src_ref=ps.at[pl.ds(pl.multiple_of(t * tile, tile), tile)],
            dst_ref=rbuf.at[k - 1], send_sem=r_send.at[k - 1], recv_sem=r_recv.at[k - 1],
            device_id=dev(t), device_id_type=MESH,
        )

    @pl.loop(1, n)
    def _(k):
        reduce_copy(k).start()

    for dx, dy in DIRS:
        @pl.when(present(dx, dy))
        def _(dx=dx, dy=dy):
            for c in copies(dx, dy):
                c.wait_send()

    @pl.loop(1, n)
    def _(k):
        reduce_copy(k).wait()

    total = ps[pl.ds(pl.multiple_of(me * tile, tile), tile), :]
    total = total + jnp.sum(rbuf[...], axis=0)
    for r in range(tile // groups):
        for q in range(groups):
            rep[r : r + 1, q * LANES : (q + 1) * LANES] = total[
                r * groups + q : r * groups + q + 1
            ]


def solution(mesh):
    nx, ny = mesh.shape["gx"], mesh.shape["gy"]
    n = nx * ny

    def per_device(adjoint, conduct_x, conduct_y, pick_weights, owner_order):
        cx, cy, cols = adjoint.shape
        picks = pick_weights.shape[0]
        groups = cols // LANES
        ex, ey = cx + 2 * STEPS, cy + SUB
        tile = picks // n * groups
        vmem = pl.BlockSpec(memory_space=pltpu.VMEM)
        dma = pltpu.SemaphoreType.DMA
        return pl.pallas_call(
            functools.partial(kernel, nx, ny),
            out_shape=(
                jax.ShapeDtypeStruct((cx, cy, cols), BF16),
                jax.ShapeDtypeStruct((picks // n, cols), F32),
            ),
            in_specs=[pl.BlockSpec(memory_space=pl.ANY)] + [vmem] * 4,
            out_specs=(vmem, vmem),
            scratch_shapes=[
                pltpu.VMEM((ex, cy, cols), BF16),
                pltpu.VMEM((2, ex, SUB, cols), BF16),
                pltpu.VMEM((len(DIRS), 2, cx, cy), F32),
                pltpu.VMEM((ex, ey, LANES), F32),
                pltpu.VMEM((ex, ey, LANES), F32),
                pltpu.VMEM((STEPS, groups, ex, ey, LANES), F32),
                pltpu.VMEM((picks * cx, LANES), F32),
                pltpu.VMEM((picks, cx * cy), BF16),
                pltpu.VMEM((picks * groups, LANES), F32),
                pltpu.VMEM((n - 1, tile, LANES), F32),
                dma,
                dma((len(DIRS), groups)),
                dma((len(DIRS), groups)),
                dma((len(DIRS), 2)),
                dma((len(DIRS), 2)),
                dma((n - 1,)),
                dma((n - 1,)),
            ],
            compiler_params=pltpu.CompilerParams(
                collective_id=0, has_side_effects=True, vmem_limit_bytes=56 << 20
            ),
        )(adjoint, conduct_x, conduct_y, pick_weights, owner_order.reshape(1, picks))

    return jax.shard_map(
        per_device,
        mesh=mesh,
        in_specs=(P("gx", "gy", None), P("gx", "gy"), P("gx", "gy"), P(None, "gx", "gy"), P()),
        out_specs=(P("gx", "gy", None), P(("gx", "gy"), None)),
        check_vma=False,
    )
```

```python
import functools

import jax
import jax.numpy as jnp
from jax import lax
from jax.experimental import pallas as pl
from jax.experimental.pallas import tpu as pltpu
from jax.sharding import PartitionSpec as P

STEPS = 4
LANES = 128
SUB = 8
MESH = pl.DeviceIdType.MESH
DIRS = ((0, 1), (0, -1), (1, 1), (1, -1), (-1, 1), (-1, -1), (1, 0), (-1, 0))
F32 = jnp.float32
BF16 = jnp.bfloat16


def dir_id(dx, dy):
    return DIRS.index((dx, dy))


def kernel(
    nx, ny, adj, kx_ref, ky_ref, w_ref, order_ref, out_hbm, rep,
    out, eb, yb, kn, kxb, kyb, u, w32, wt, ps, rbuf,
    load_sem, out_sem, a_send, a_recv, k_send, k_recv, r_send, r_recv,
):
    cx, cy, cols = adj.shape
    groups = cols // LANES
    ex = cx + 2 * STEPS
    ey = cy + SUB
    picks = w_ref.shape[0]
    n = nx * ny
    tile = ps.shape[0] // n
    gx = lax.axis_index("gx")
    gy = lax.axis_index("gy")
    me = gx * ny + gy

    def dev(t):
        return (t // ny, lax.rem(t, ny))

    barrier = pltpu.get_barrier_semaphore()

    @pl.loop(1, n)
    def _(k):
        pl.semaphore_signal(
            barrier, inc=1, device_id=dev(lax.rem(me + k, n)), device_id_type=MESH
        )

    own = pltpu.make_async_copy(adj, eb.at[pl.ds(STEPS, cx)], load_sem)
    own.start()

    def present(dx, dy):
        ok = None
        for d, g, size in ((dx, gx, nx), (dy, gy, ny)):
            if d == 1:
                c = g < size - 1
            elif d == -1:
                c = g > 0
            else:
                continue
            ok = c if ok is None else jnp.logical_and(ok, c)
        return ok

    def region(sx, sy):
        rows = {-1: pl.ds(0, STEPS), 0: pl.ds(STEPS, cx), 1: pl.ds(STEPS + cx, STEPS)}[sx]
        if sy == 0:
            return eb.at[rows]
        return yb.at[0 if sy == 1 else 1, rows]

    def copies(dx, dy):
        sx, sy = -dx, -dy
        slot, mine = dir_id(sx, sy), dir_id(dx, dy)
        target = (gx + dx, gy + dy)
        src = adj
        if dx:
            src = src.at[pl.ds(cx - STEPS if dx == 1 else 0, STEPS)]
        if dy:
            src = src.at[:, pl.ds(cy - SUB if dy == 1 else 0, SUB)]
        dst = region(sx, sy)
        result = []
        for a, kref in enumerate((kx_ref, ky_ref)):
            result.append(
                pltpu.make_async_remote_copy(
                    src_ref=kref, dst_ref=kn.at[slot, a], send_sem=k_send.at[mine, a],
                    recv_sem=k_recv.at[slot, a], device_id=target, device_id_type=MESH,
                )
            )
        parts = [(src, dst)]
        if dy == 0:
            parts = [
                (src.at[:, :, pl.ds(q * LANES, LANES)], dst.at[:, :, pl.ds(q * LANES, LANES)])
                for q in range(groups)
            ]
        for q, (s, d) in enumerate(parts):
            result.append(
                pltpu.make_async_remote_copy(
                    src_ref=s, dst_ref=d, send_sem=a_send.at[mine, q],
                    recv_sem=a_recv.at[slot, q], device_id=target, device_id_type=MESH,
                )
            )
        return result

    pick_ids = lax.broadcasted_iota(jnp.int32, (picks, picks), 0)
    chosen = jnp.where(pick_ids == order_ref[...], F32(1), F32(0)).astype(BF16)
    w32[...] = w_ref[...].astype(F32).reshape(picks * cx, LANES)

    def sort_weights():
        for x in range(cx):
            row = w32[pl.ds(x, picks, stride=cx), :].astype(BF16)
            row = lax.dot_general(
                chosen, row, (((0,), (0,)), ((), ())), preferred_element_type=F32
            )
            wt[:, x * LANES : (x + 1) * LANES] = row.astype(BF16)

    def lanes(q):
        if isinstance(q, int):
            return pl.ds(q * LANES, LANES)
        return pl.ds(pl.multiple_of(q * LANES, LANES), LANES)

    def widen(q, lo, hi):
        @pl.loop(lo, hi)
        def _(e):
            u[0, q, e, :cy] = eb[e, :, lanes(q)].astype(F32)

    sort_weights()
    own.wait()

    @pl.loop(0, groups)
    def _(q):
        widen(q, STEPS, STEPS + cx)

    pl.semaphore_wait(barrier, n - 1)

    for dx, dy in DIRS:
        @pl.when(present(dx, dy))
        def _(dx=dx, dy=dy):
            for c in copies(dx, dy):
                c.start()

        @pl.when(jnp.logical_not(present(dx, dy)))
        def _(dx=dx, dy=dy):
            part = region(dx, dy)
            part[...] = jnp.zeros(part.shape, BF16)
            kn[dir_id(dx, dy)] = jnp.zeros(kn.shape[1:], F32)

    def wait_recv(dx, dy, what):
        @pl.when(present(dx, dy))
        def _():
            slot = dir_id(dx, dy)
            if what == "k":
                for a in range(2):
                    pltpu.make_async_copy(kn.at[slot, a], kn.at[slot, a], k_recv.at[slot, a]).wait()
            elif what == "a":
                part = region(dx, dy)
                pltpu.make_async_copy(part, part, a_recv.at[slot, 0]).wait()
            else:
                part = region(dx, dy).at[:, :, pl.ds(what * LANES, LANES)]
                pltpu.make_async_copy(part, part, a_recv.at[slot, what]).wait()

    for d in DIRS:
        wait_recv(*d, "k")

    low = lax.broadcasted_iota(jnp.int32, (SUB, cx), 0) < STEPS
    place = lax.broadcasted_iota(jnp.int32, (ey, cx), 0)
    for a, (kref, store) in enumerate(((kx_ref, kxb), (ky_ref, kyb))):
        for sx in (-1, 0, 1):
            def block(sy):
                if sx == 0 and sy == 0:
                    return kref[...]
                return kn[dir_id(sx, sy), a]

            main = block(0).T
            tail = jnp.where(low, block(1).T[:SUB], block(-1).T[cy - SUB :])
            whole = jnp.concatenate([main, tail], axis=0)
            if a == 1:
                whole = jnp.where(
                    jnp.logical_and(place == cy - 1, gy == ny - 1), F32(0), whole
                )
            rows = {-1: range(cx - STEPS, cx), 0: range(cx), 1: range(STEPS)}[sx]
            base = {-1: 0, 0: STEPS, 1: STEPS + cx}[sx]
            for i, r in enumerate(rows):
                column = jnp.broadcast_to(whole[:, r : r + 1], (ey, LANES))
                if a == 0 and sx == 0 and r == cx - 1:
                    column = jnp.where(gx == nx - 1, F32(0), column)
                store[base + i] = column

    low_lane = lax.broadcasted_iota(jnp.int32, (SUB, LANES), 0) < STEPS

    def fringe(q, lo, hi):
        @pl.loop(lo, hi)
        def _(e):
            right = yb[0, e, :, lanes(q)].astype(F32)
            left = yb[1, e, :, lanes(q)].astype(F32)
            u[0, q, e, cy:] = jnp.where(low_lane, right, left)

    def sweep(level, q, lo, hi):
        here = u[level, q, lo]
        before = kxb[lo - 1] * (here - u[level, q, lo - 1])

        def body(e, carry):
            here, before = carry
            below = u[level, q, e + 1]
            after = kxb[e] * (below - here)
            side = kyb[e] * (pltpu.roll(here, ey - 1, 0) - here)
            value = (here + (after - before)) + (side - pltpu.roll(side, 1, 0))
            if level < STEPS - 1:
                u[level + 1, q, e] = value
            else:
                out[e - STEPS, :, lanes(q)] = value[:cy].astype(BF16)
            return below, after

        lax.fori_loop(lo, hi, body, (here, before))

    def product(lo, hi):
        return jnp.dot(
            wt[:, lo * LANES : hi * LANES],
            out[lo:hi].reshape((hi - lo) * cy, cols),
            preferred_element_type=F32,
        )

    for d in DIRS[:2]:
        wait_recv(*d, "a")

    @pl.loop(0, groups)
    def _(q):
        fringe(q, STEPS, STEPS + cx)
        for s in range(1, STEPS + 1):
            sweep(s - 1, q, STEPS + s, STEPS + cx - s)

    for d in DIRS[2:6]:
        wait_recv(*d, "a")
    for q in range(groups):
        for d in DIRS[6:]:
            wait_recv(*d, q)
        for lo in (0, STEPS + cx):
            widen(q, lo, lo + STEPS)
            fringe(q, lo, lo + STEPS)
        for s in range(1, STEPS + 1):
            sweep(s - 1, q, s, STEPS + s)
            sweep(s - 1, q, STEPS + cx - s, ex - s)

    store = pltpu.make_async_copy(out, out_hbm, out_sem)
    store.start()
    total = product(0, cx)
    for q in range(groups):
        ps[pl.ds(q, picks, stride=groups), :] = total[:, q * LANES : (q + 1) * LANES]

    def reduce_copy(k):
        t = lax.rem(me + k, n)
        return pltpu.make_async_remote_copy(
            src_ref=ps.at[pl.ds(pl.multiple_of(t * tile, tile), tile)],
            dst_ref=rbuf.at[k - 1], send_sem=r_send.at[k - 1], recv_sem=r_recv.at[k - 1],
            device_id=dev(t), device_id_type=MESH,
        )

    @pl.loop(1, n)
    def _(k):
        reduce_copy(k).start()

    for dx, dy in DIRS:
        @pl.when(present(dx, dy))
        def _(dx=dx, dy=dy):
            for c in copies(dx, dy):
                c.wait_send()

    @pl.loop(1, n)
    def _(k):
        reduce_copy(k).wait()

    total = ps[pl.ds(pl.multiple_of(me * tile, tile), tile), :]
    total = total + jnp.sum(rbuf[...], axis=0)
    for r in range(tile // groups):
        for q in range(groups):
            rep[r : r + 1, q * LANES : (q + 1) * LANES] = total[
                r * groups + q : r * groups + q + 1
            ]
    store.wait()


def copy_kernel(src, small, dst, small_dst, buf, sem_in, sem_out):
    small_dst[...] = small[...]
    parts = buf.shape[0]
    rows = src.shape[0] // parts

    def moves(i):
        own = pl.ds(i * rows, rows)
        return (
            pltpu.make_async_copy(src.at[own], buf.at[i], sem_in.at[i]),
            pltpu.make_async_copy(buf.at[i], dst.at[own], sem_out.at[i]),
        )

    for i in range(parts):
        moves(i)[0].start()
    for i in range(parts):
        moves(i)[0].wait()
        moves(i)[1].start()
    for i in range(parts):
        moves(i)[1].wait()


def solution(mesh):
    nx, ny = mesh.shape["gx"], mesh.shape["gy"]
    n = nx * ny

    def per_device(adjoint, conduct_x, conduct_y, pick_weights, owner_order):
        cx, cy, cols = adjoint.shape
        picks = pick_weights.shape[0]
        groups = cols // LANES
        ex, ey = cx + 2 * STEPS, cy + SUB
        tile = picks // n * groups
        vmem = pl.BlockSpec(memory_space=pltpu.VMEM)
        dma = pltpu.SemaphoreType.DMA
        any_space = pl.BlockSpec(memory_space=pl.ANY)
        smoothed, owned = pl.pallas_call(
            functools.partial(kernel, nx, ny),
            out_shape=(
                jax.ShapeDtypeStruct((cx, cy, cols), BF16),
                jax.ShapeDtypeStruct((picks // n, cols), F32),
            ),
            in_specs=[any_space] + [vmem] * 4,
            out_specs=(any_space, vmem),
            scratch_shapes=[
                pltpu.VMEM((cx, cy, cols), BF16),
                pltpu.VMEM((ex, cy, cols), BF16),
                pltpu.VMEM((2, ex, SUB, cols), BF16),
                pltpu.VMEM((len(DIRS), 2, cx, cy), F32),
                pltpu.VMEM((ex, ey, LANES), F32),
                pltpu.VMEM((ex, ey, LANES), F32),
                pltpu.VMEM((STEPS, groups, ex, ey, LANES), F32),
                pltpu.VMEM((picks * cx, LANES), F32),
                pltpu.VMEM((picks, cx * cy), BF16),
                pltpu.VMEM((picks * groups, LANES), F32),
                pltpu.VMEM((n - 1, tile, LANES), F32),
                dma,
                dma,
                dma((len(DIRS), groups)),
                dma((len(DIRS), groups)),
                dma((len(DIRS), 2)),
                dma((len(DIRS), 2)),
                dma((n - 1,)),
                dma((n - 1,)),
            ],
            compiler_params=pltpu.CompilerParams(
                collective_id=0, has_side_effects=True, vmem_limit_bytes=56 << 20
            ),
        )(adjoint, conduct_x, conduct_y, pick_weights, owner_order.reshape(1, picks))
        parts = 4
        return pl.pallas_call(
            copy_kernel,
            out_shape=(
                jax.ShapeDtypeStruct((cx, cy, cols), BF16),
                jax.ShapeDtypeStruct((picks // n, cols), F32),
            ),
            in_specs=[any_space, vmem],
            out_specs=(any_space, vmem),
            scratch_shapes=[
                pltpu.VMEM((parts, cx // parts, cy, cols), BF16),
                dma((parts,)),
                dma((parts,)),
            ],
        )(smoothed, owned)

    return jax.shard_map(
        per_device,
        mesh=mesh,
        in_specs=(P("gx", "gy", None), P("gx", "gy"), P("gx", "gy"), P(None, "gx", "gy"), P()),
        out_specs=(P("gx", "gy", None), P(("gx", "gy"), None)),
        check_vma=False,
    )
```

```python
import functools

import jax
import jax.numpy as jnp
from jax import lax
from jax.experimental import pallas as pl
from jax.experimental.pallas import tpu as pltpu
from jax.sharding import PartitionSpec as P

STEPS = 4
LANES = 128
SUB = 8
MESH = pl.DeviceIdType.MESH
DIRS = ((0, 1), (0, -1), (1, 1), (1, -1), (-1, 1), (-1, -1), (1, 0), (-1, 0))
F32 = jnp.float32
BF16 = jnp.bfloat16


def dir_id(dx, dy):
    return DIRS.index((dx, dy))


def kernel(
    nx, ny, adj, kx_ref, ky_ref, w_ref, order_ref, out_hbm, rep,
    out, eb, yb, kn, kxb, kyb, u, w32, wt, ps, rbuf,
    load_sem, out_sem, a_send, a_recv, k_send, k_recv, r_send, r_recv,
):
    cx, cy, cols = adj.shape
    groups = cols // LANES
    ex = cx + 2 * STEPS
    ey = cy + SUB
    picks = w_ref.shape[0]
    n = nx * ny
    tile = ps.shape[0] // n
    gx = lax.axis_index("gx")
    gy = lax.axis_index("gy")
    me = gx * ny + gy

    def dev(t):
        return (t // ny, lax.rem(t, ny))

    barrier = pltpu.get_barrier_semaphore()

    @pl.loop(1, n)
    def _(k):
        pl.semaphore_signal(
            barrier, inc=1, device_id=dev(lax.rem(me + k, n)), device_id_type=MESH
        )

    own = pltpu.make_async_copy(adj, eb.at[pl.ds(STEPS, cx)], load_sem)
    own.start()

    def present(dx, dy):
        ok = None
        for d, g, size in ((dx, gx, nx), (dy, gy, ny)):
            if d == 1:
                c = g < size - 1
            elif d == -1:
                c = g > 0
            else:
                continue
            ok = c if ok is None else jnp.logical_and(ok, c)
        return ok

    def region(sx, sy):
        rows = {-1: pl.ds(0, STEPS), 0: pl.ds(STEPS, cx), 1: pl.ds(STEPS + cx, STEPS)}[sx]
        if sy == 0:
            return eb.at[rows]
        return yb.at[0 if sy == 1 else 1, rows]

    def copies(dx, dy):
        sx, sy = -dx, -dy
        slot, mine = dir_id(sx, sy), dir_id(dx, dy)
        target = (gx + dx, gy + dy)
        src = adj
        if dx:
            src = src.at[pl.ds(cx - STEPS if dx == 1 else 0, STEPS)]
        if dy:
            src = src.at[:, pl.ds(cy - SUB if dy == 1 else 0, SUB)]
        dst = region(sx, sy)
        result = []
        for a, kref in enumerate((kx_ref, ky_ref)):
            result.append(
                pltpu.make_async_remote_copy(
                    src_ref=kref, dst_ref=kn.at[slot, a], send_sem=k_send.at[mine, a],
                    recv_sem=k_recv.at[slot, a], device_id=target, device_id_type=MESH,
                )
            )
        parts = [(src, dst)]
        if dy == 0:
            parts = [
                (src.at[:, :, pl.ds(q * LANES, LANES)], dst.at[:, :, pl.ds(q * LANES, LANES)])
                for q in range(groups)
            ]
        for q, (s, d) in enumerate(parts):
            result.append(
                pltpu.make_async_remote_copy(
                    src_ref=s, dst_ref=d, send_sem=a_send.at[mine, q],
                    recv_sem=a_recv.at[slot, q], device_id=target, device_id_type=MESH,
                )
            )
        return result

    pick_ids = lax.broadcasted_iota(jnp.int32, (picks, picks), 0)
    chosen = jnp.where(pick_ids == order_ref[...], F32(1), F32(0)).astype(BF16)
    w32[...] = w_ref[...].astype(F32).reshape(picks * cx, LANES)

    def sort_weights():
        for x in range(cx):
            row = w32[pl.ds(x, picks, stride=cx), :].astype(BF16)
            row = lax.dot_general(
                chosen, row, (((0,), (0,)), ((), ())), preferred_element_type=F32
            )
            wt[:, x * LANES : (x + 1) * LANES] = row.astype(BF16)

    def lanes(q):
        if isinstance(q, int):
            return pl.ds(q * LANES, LANES)
        return pl.ds(pl.multiple_of(q * LANES, LANES), LANES)

    def widen(q, lo, hi):
        @pl.loop(lo, hi)
        def _(e):
            u[0, q, e, :cy] = eb[e, :, lanes(q)].astype(F32)

    place = lax.broadcasted_iota(jnp.int32, (cy, cx), 0)

    def own_k(a, block):
        main = block.T
        if a == 1:
            edge = jnp.logical_and(place == cy - 1, gy == ny - 1)
            main = jnp.where(edge, F32(0), main)
        return main

    for a, (kref, kstore) in enumerate(((kx_ref, kxb), (ky_ref, kyb))):
        main = own_k(a, kref[...])
        for r in range(cx):
            column = jnp.broadcast_to(main[:, r : r + 1], (cy, LANES))
            if a == 0 and r == cx - 1:
                column = jnp.where(gx == nx - 1, F32(0), column)
            kstore[STEPS + r, :cy] = column

    own.wait()

    @pl.loop(0, groups)
    def _(q):
        widen(q, STEPS, STEPS + cx)

    pl.semaphore_wait(barrier, n - 1)

    for dx, dy in DIRS:
        @pl.when(present(dx, dy))
        def _(dx=dx, dy=dy):
            for c in copies(dx, dy):
                c.start()

        @pl.when(jnp.logical_not(present(dx, dy)))
        def _(dx=dx, dy=dy):
            part = region(dx, dy)
            part[...] = jnp.zeros(part.shape, BF16)
            kn[dir_id(dx, dy)] = jnp.zeros(kn.shape[1:], F32)

    def wait_recv(dx, dy, what):
        @pl.when(present(dx, dy))
        def _():
            slot = dir_id(dx, dy)
            if what == "k":
                for a in range(2):
                    pltpu.make_async_copy(kn.at[slot, a], kn.at[slot, a], k_recv.at[slot, a]).wait()
            elif what == "a":
                part = region(dx, dy)
                pltpu.make_async_copy(part, part, a_recv.at[slot, 0]).wait()
            else:
                part = region(dx, dy).at[:, :, pl.ds(what * LANES, LANES)]
                pltpu.make_async_copy(part, part, a_recv.at[slot, what]).wait()

    low_lane = lax.broadcasted_iota(jnp.int32, (SUB, LANES), 0) < STEPS

    def fringe(q, lo, hi):
        @pl.loop(lo, hi)
        def _(e):
            right = yb[0, e, :, lanes(q)].astype(F32)
            left = yb[1, e, :, lanes(q)].astype(F32)
            u[0, q, e, cy:] = jnp.where(low_lane, right, left)

    def sweep(level, q, lo, hi, wide=ey):
        own_cols = pl.ds(0, wide)
        here = u[level, q, lo, own_cols]
        before = kxb[lo - 1, own_cols] * (here - u[level, q, lo - 1, own_cols])

        def body(e, carry):
            here, before = carry
            below = u[level, q, e + 1, own_cols]
            after = kxb[e, own_cols] * (below - here)
            side = kyb[e, own_cols] * (pltpu.roll(here, wide - 1, 0) - here)
            value = (here + (after - before)) + (side - pltpu.roll(side, 1, 0))
            if level < STEPS - 1:
                u[level + 1, q, e, own_cols] = value
            else:
                out[e - STEPS, :, lanes(q)] = value[:cy].astype(BF16)
            return below, after

        lax.fori_loop(lo, hi, body, (here, before))

    def product(lo, hi):
        return jnp.dot(
            wt[:, lo * LANES : hi * LANES],
            out[lo:hi].reshape((hi - lo) * cy, cols),
            preferred_element_type=F32,
        )

    @pl.loop(0, groups)
    def _(q):
        for s in range(1, STEPS + 1):
            sweep(s - 1, q, STEPS + s, STEPS + cx - s, cy)

    sort_weights()

    for d in DIRS:
        wait_recv(*d, "k")

    low = lax.broadcasted_iota(jnp.int32, (SUB, cx), 0) < STEPS
    for a, store in enumerate((kxb, kyb)):
        for sx in (-1, 0, 1):
            tail = jnp.where(
                low,
                kn[dir_id(sx, 1), a].T[:SUB],
                kn[dir_id(sx, -1), a].T[cy - SUB :],
            )
            main = None if sx == 0 else own_k(a, kn[dir_id(sx, 0), a])
            rows = {-1: range(cx - STEPS, cx), 0: range(cx), 1: range(STEPS)}[sx]
            base = {-1: 0, 0: STEPS, 1: STEPS + cx}[sx]
            for i, r in enumerate(rows):
                column = jnp.broadcast_to(tail[:, r : r + 1], (SUB, LANES))
                if a == 0 and sx == 0 and r == cx - 1:
                    column = jnp.where(gx == nx - 1, F32(0), column)
                store[base + i, cy:] = column
                if sx:
                    store[base + i, :cy] = jnp.broadcast_to(main[:, r : r + 1], (cy, LANES))

    for d in DIRS[:2]:
        wait_recv(*d, "a")

    @pl.loop(0, groups)
    def _(q):
        fringe(q, STEPS, STEPS + cx)

    def strips(level, lo, hi):
        span = 3 * SUB

        def window(get):
            return jnp.concatenate(
                [get(pl.ds(cy - SUB, 2 * SUB)), get(pl.ds(0, SUB))], axis=0
            )

        @pl.loop(lo, hi)
        def _(e):
            up = window(lambda c: kxb[e - 1, c])
            down = window(lambda c: kxb[e, c])
            along = window(lambda c: kyb[e, c])
            for q in range(groups):
                here = window(lambda c: u[level, q, e, c])
                above = window(lambda c: u[level, q, e - 1, c])
                below = window(lambda c: u[level, q, e + 1, c])
                flow = down * (below - here) - up * (here - above)
                side = along * (pltpu.roll(here, span - 1, 0) - here)
                value = (here + flow) + (side - pltpu.roll(side, 1, 0))
                first, mid, last = (value[i * SUB : (i + 1) * SUB] for i in range(3))
                if level < STEPS - 1:
                    head = u[level + 1, q, e, cy - SUB : cy]
                    foot = u[level + 1, q, e, :SUB]
                    u[level + 1, q, e, cy - SUB : cy] = jnp.where(low_lane, head, first)
                    u[level + 1, q, e, cy:] = mid
                    u[level + 1, q, e, :SUB] = jnp.where(low_lane, last, foot)
                else:
                    head = out[e - STEPS, cy - SUB :, lanes(q)].astype(F32)
                    foot = out[e - STEPS, :SUB, lanes(q)].astype(F32)
                    out[e - STEPS, cy - SUB :, lanes(q)] = jnp.where(
                        low_lane, head, first
                    ).astype(BF16)
                    out[e - STEPS, :SUB, lanes(q)] = jnp.where(
                        low_lane, last, foot
                    ).astype(BF16)

    for s in range(1, STEPS + 1):
        strips(s - 1, STEPS + s, STEPS + cx - s)

    for d in DIRS[2:6]:
        wait_recv(*d, "a")
    for q in range(groups):
        for d in DIRS[6:]:
            wait_recv(*d, q)
        for lo in (0, STEPS + cx):
            widen(q, lo, lo + STEPS)
            fringe(q, lo, lo + STEPS)
        for s in range(1, STEPS + 1):
            sweep(s - 1, q, s, STEPS + s)
            sweep(s - 1, q, STEPS + cx - s, ex - s)

    store = pltpu.make_async_copy(out, out_hbm, out_sem)
    store.start()
    total = product(0, cx)
    for q in range(groups):
        ps[pl.ds(q, picks, stride=groups), :] = total[:, q * LANES : (q + 1) * LANES]

    def reduce_copy(k):
        t = lax.rem(me + k, n)
        return pltpu.make_async_remote_copy(
            src_ref=ps.at[pl.ds(pl.multiple_of(t * tile, tile), tile)],
            dst_ref=rbuf.at[k - 1], send_sem=r_send.at[k - 1], recv_sem=r_recv.at[k - 1],
            device_id=dev(t), device_id_type=MESH,
        )

    @pl.loop(1, n)
    def _(k):
        reduce_copy(k).start()

    for dx, dy in DIRS:
        @pl.when(present(dx, dy))
        def _(dx=dx, dy=dy):
            for c in copies(dx, dy):
                c.wait_send()

    @pl.loop(1, n)
    def _(k):
        reduce_copy(k).wait()

    total = ps[pl.ds(pl.multiple_of(me * tile, tile), tile), :]
    total = total + jnp.sum(rbuf[...], axis=0)
    for r in range(tile // groups):
        for q in range(groups):
            rep[r : r + 1, q * LANES : (q + 1) * LANES] = total[
                r * groups + q : r * groups + q + 1
            ]
    store.wait()


def solution(mesh):
    nx, ny = mesh.shape["gx"], mesh.shape["gy"]
    n = nx * ny

    def per_device(adjoint, conduct_x, conduct_y, pick_weights, owner_order):
        cx, cy, cols = adjoint.shape
        picks = pick_weights.shape[0]
        groups = cols // LANES
        ex, ey = cx + 2 * STEPS, cy + SUB
        tile = picks // n * groups
        vmem = pl.BlockSpec(memory_space=pltpu.VMEM)
        dma = pltpu.SemaphoreType.DMA
        any_space = pl.BlockSpec(memory_space=pl.ANY)
        smoothed, owned = pl.pallas_call(
            functools.partial(kernel, nx, ny),
            out_shape=(
                jax.ShapeDtypeStruct((cx, cy, cols), BF16),
                jax.ShapeDtypeStruct((picks // n, cols), F32),
            ),
            in_specs=[any_space] + [vmem] * 4,
            out_specs=(any_space, vmem),
            scratch_shapes=[
                pltpu.VMEM((cx, cy, cols), BF16),
                pltpu.VMEM((ex, cy, cols), BF16),
                pltpu.VMEM((2, ex, SUB, cols), BF16),
                pltpu.VMEM((len(DIRS), 2, cx, cy), F32),
                pltpu.VMEM((ex, ey, LANES), F32),
                pltpu.VMEM((ex, ey, LANES), F32),
                pltpu.VMEM((STEPS, groups, ex, ey, LANES), F32),
                pltpu.VMEM((picks * cx, LANES), F32),
                pltpu.VMEM((picks, cx * cy), BF16),
                pltpu.VMEM((picks * groups, LANES), F32),
                pltpu.VMEM((n - 1, tile, LANES), F32),
                dma,
                dma,
                dma((len(DIRS), groups)),
                dma((len(DIRS), groups)),
                dma((len(DIRS), 2)),
                dma((len(DIRS), 2)),
                dma((n - 1,)),
                dma((n - 1,)),
            ],
            compiler_params=pltpu.CompilerParams(
                collective_id=0, has_side_effects=True, vmem_limit_bytes=56 << 20
            ),
        )(adjoint, conduct_x, conduct_y, pick_weights, owner_order.reshape(1, picks))
        return smoothed, owned

    return jax.shard_map(
        per_device,
        mesh=mesh,
        in_specs=(P("gx", "gy", None), P("gx", "gy"), P("gx", "gy"), P(None, "gx", "gy"), P()),
        out_specs=(P("gx", "gy", None), P(("gx", "gy"), None)),
        check_vma=False,
    )
```

```python
import functools

import jax
import jax.numpy as jnp
from jax import lax
from jax.experimental import pallas as pl
from jax.experimental.pallas import tpu as pltpu
from jax.sharding import PartitionSpec as P

STEPS = 4
LANES = 128
SUB = 8
MESH = pl.DeviceIdType.MESH
DIRS = ((0, 1), (0, -1), (1, 1), (1, -1), (-1, 1), (-1, -1), (1, 0), (-1, 0))
F32 = jnp.float32
BF16 = jnp.bfloat16


def dir_id(dx, dy):
    return DIRS.index((dx, dy))


def kernel(
    nx, ny, adj, kx_ref, ky_ref, w_ref, order_ref, out_hbm, rep,
    out, eb, yb, kn, kxb, kyb, u, w32, wt, ps, rbuf,
    load_sem, out_sem, a_send, a_recv, k_send, k_recv, r_send, r_recv,
):
    cx, cy, cols = adj.shape
    groups = cols // LANES
    ex = cx + 2 * STEPS
    ey = cy + SUB
    picks = w_ref.shape[0]
    n = nx * ny
    tile = ps.shape[0] // n
    gx = lax.axis_index("gx")
    gy = lax.axis_index("gy")
    me = gx * ny + gy

    def dev(t):
        return (t // ny, lax.rem(t, ny))

    barrier = pltpu.get_barrier_semaphore()

    @pl.loop(1, n)
    def _(k):
        pl.semaphore_signal(
            barrier, inc=1, device_id=dev(lax.rem(me + k, n)), device_id_type=MESH
        )

    own = pltpu.make_async_copy(adj, eb.at[pl.ds(STEPS, cx)], load_sem)
    own.start()

    def present(dx, dy):
        ok = None
        for d, g, size in ((dx, gx, nx), (dy, gy, ny)):
            if d == 1:
                c = g < size - 1
            elif d == -1:
                c = g > 0
            else:
                continue
            ok = c if ok is None else jnp.logical_and(ok, c)
        return ok

    def region(sx, sy):
        rows = {-1: pl.ds(0, STEPS), 0: pl.ds(STEPS, cx), 1: pl.ds(STEPS + cx, STEPS)}[sx]
        if sy == 0:
            return eb.at[rows]
        return yb.at[0 if sy == 1 else 1, rows]

    def copies(dx, dy):
        sx, sy = -dx, -dy
        slot, mine = dir_id(sx, sy), dir_id(dx, dy)
        target = (gx + dx, gy + dy)
        src = adj
        if dx:
            src = src.at[pl.ds(cx - STEPS if dx == 1 else 0, STEPS)]
        if dy:
            src = src.at[:, pl.ds(cy - SUB if dy == 1 else 0, SUB)]
        dst = region(sx, sy)
        result = []
        for a, kref in enumerate((kx_ref, ky_ref)):
            result.append(
                pltpu.make_async_remote_copy(
                    src_ref=kref, dst_ref=kn.at[slot, a], send_sem=k_send.at[mine, a],
                    recv_sem=k_recv.at[slot, a], device_id=target, device_id_type=MESH,
                )
            )
        parts = [(src, dst)]
        if dy == 0:
            parts = [
                (src.at[:, :, pl.ds(q * LANES, LANES)], dst.at[:, :, pl.ds(q * LANES, LANES)])
                for q in range(groups)
            ]
        for q, (s, d) in enumerate(parts):
            result.append(
                pltpu.make_async_remote_copy(
                    src_ref=s, dst_ref=d, send_sem=a_send.at[mine, q],
                    recv_sem=a_recv.at[slot, q], device_id=target, device_id_type=MESH,
                )
            )
        return result

    pick_ids = lax.broadcasted_iota(jnp.int32, (picks, picks), 0)
    chosen = jnp.where(pick_ids == order_ref[...], F32(1), F32(0)).astype(BF16)
    w32[...] = w_ref[...].astype(F32).reshape(picks * cx, LANES)

    def sort_weights():
        for x in range(cx):
            row = w32[pl.ds(x, picks, stride=cx), :].astype(BF16)
            row = lax.dot_general(
                chosen, row, (((0,), (0,)), ((), ())), preferred_element_type=F32
            )
            wt[:, x * LANES : (x + 1) * LANES] = row.astype(BF16)

    def lanes(q):
        if isinstance(q, int):
            return pl.ds(q * LANES, LANES)
        return pl.ds(pl.multiple_of(q * LANES, LANES), LANES)

    def widen(q, lo, hi):
        @pl.loop(lo, hi)
        def _(e):
            u[0, q, e, :cy] = eb[e, :, lanes(q)].astype(F32)

    place = lax.broadcasted_iota(jnp.int32, (cy, cx), 0)

    def own_k(a, block):
        main = block.T
        if a == 1:
            edge = jnp.logical_and(place == cy - 1, gy == ny - 1)
            main = jnp.where(edge, F32(0), main)
        return main

    for a, (kref, kstore) in enumerate(((kx_ref, kxb), (ky_ref, kyb))):
        main = own_k(a, kref[...])
        for r in range(cx):
            column = jnp.broadcast_to(main[:, r : r + 1], (cy, LANES))
            if a == 0 and r == cx - 1:
                column = jnp.where(gx == nx - 1, F32(0), column)
            kstore[STEPS + r, :cy] = column

    own.wait()

    @pl.loop(0, groups)
    def _(q):
        widen(q, STEPS, STEPS + cx)

    pl.semaphore_wait(barrier, n - 1)

    order = [(d, 0, 2) for d in DIRS] + [(d, 2, 3) for d in DIRS[:6]]
    order += [(d, 2 + q, 3 + q) for q in range(groups) for d in DIRS[6:]]
    for (dx, dy), first, last in order:
        @pl.when(present(dx, dy))
        def _(dx=dx, dy=dy, first=first, last=last):
            for c in copies(dx, dy)[first:last]:
                c.start()

    for dx, dy in DIRS:
        @pl.when(jnp.logical_not(present(dx, dy)))
        def _(dx=dx, dy=dy):
            part = region(dx, dy)
            part[...] = jnp.zeros(part.shape, BF16)
            kn[dir_id(dx, dy)] = jnp.zeros(kn.shape[1:], F32)

    def wait_recv(dx, dy, what):
        @pl.when(present(dx, dy))
        def _():
            slot = dir_id(dx, dy)
            if what == "k":
                for a in range(2):
                    pltpu.make_async_copy(kn.at[slot, a], kn.at[slot, a], k_recv.at[slot, a]).wait()
            elif what == "a":
                part = region(dx, dy)
                pltpu.make_async_copy(part, part, a_recv.at[slot, 0]).wait()
            else:
                part = region(dx, dy).at[:, :, pl.ds(what * LANES, LANES)]
                pltpu.make_async_copy(part, part, a_recv.at[slot, what]).wait()

    low_lane = lax.broadcasted_iota(jnp.int32, (SUB, LANES), 0) < STEPS

    def fringe(q, lo, hi):
        @pl.loop(lo, hi)
        def _(e):
            right = yb[0, e, :, lanes(q)].astype(F32)
            left = yb[1, e, :, lanes(q)].astype(F32)
            u[0, q, e, cy:] = jnp.where(low_lane, right, left)

    def sweep(level, q, lo, hi, wide=ey):
        own_cols = pl.ds(0, wide)
        here = u[level, q, lo, own_cols]
        before = kxb[lo - 1, own_cols] * (here - u[level, q, lo - 1, own_cols])

        def body(e, carry):
            here, before = carry
            below = u[level, q, e + 1, own_cols]
            after = kxb[e, own_cols] * (below - here)
            side = kyb[e, own_cols] * (pltpu.roll(here, wide - 1, 0) - here)
            value = (here + (after - before)) + (side - pltpu.roll(side, 1, 0))
            if level < STEPS - 1:
                u[level + 1, q, e, own_cols] = value
            else:
                out[e - STEPS, :, lanes(q)] = value[:cy].astype(BF16)
            return below, after

        lax.fori_loop(lo, hi, body, (here, before))

    def product(lo, hi):
        return jnp.dot(
            wt[:, lo * LANES : hi * LANES],
            out[lo:hi].reshape((hi - lo) * cy, cols),
            preferred_element_type=F32,
        )

    @pl.loop(0, groups)
    def _(q):
        for s in range(1, STEPS + 1):
            sweep(s - 1, q, STEPS + s, STEPS + cx - s, cy)

    sort_weights()

    for d in DIRS:
        wait_recv(*d, "k")

    low = lax.broadcasted_iota(jnp.int32, (SUB, cx), 0) < STEPS
    for a, store in enumerate((kxb, kyb)):
        for sx in (-1, 0, 1):
            tail = jnp.where(
                low,
                kn[dir_id(sx, 1), a].T[:SUB],
                kn[dir_id(sx, -1), a].T[cy - SUB :],
            )
            main = None if sx == 0 else own_k(a, kn[dir_id(sx, 0), a])
            rows = {-1: range(cx - STEPS, cx), 0: range(cx), 1: range(STEPS)}[sx]
            base = {-1: 0, 0: STEPS, 1: STEPS + cx}[sx]
            for i, r in enumerate(rows):
                column = jnp.broadcast_to(tail[:, r : r + 1], (SUB, LANES))
                if a == 0 and sx == 0 and r == cx - 1:
                    column = jnp.where(gx == nx - 1, F32(0), column)
                store[base + i, cy:] = column
                if sx:
                    store[base + i, :cy] = jnp.broadcast_to(main[:, r : r + 1], (cy, LANES))

    for d in DIRS[:2]:
        wait_recv(*d, "a")

    @pl.loop(0, groups)
    def _(q):
        fringe(q, STEPS, STEPS + cx)

    def strips(level, lo, hi):
        span = 3 * SUB

        def window(get):
            return jnp.concatenate(
                [get(pl.ds(cy - SUB, 2 * SUB)), get(pl.ds(0, SUB))], axis=0
            )

        @pl.loop(lo, hi)
        def _(e):
            up = window(lambda c: kxb[e - 1, c])
            down = window(lambda c: kxb[e, c])
            along = window(lambda c: kyb[e, c])
            for q in range(groups):
                here = window(lambda c: u[level, q, e, c])
                above = window(lambda c: u[level, q, e - 1, c])
                below = window(lambda c: u[level, q, e + 1, c])
                flow = down * (below - here) - up * (here - above)
                side = along * (pltpu.roll(here, span - 1, 0) - here)
                value = (here + flow) + (side - pltpu.roll(side, 1, 0))
                first, mid, last = (value[i * SUB : (i + 1) * SUB] for i in range(3))
                if level < STEPS - 1:
                    head = u[level + 1, q, e, cy - SUB : cy]
                    foot = u[level + 1, q, e, :SUB]
                    u[level + 1, q, e, cy - SUB : cy] = jnp.where(low_lane, head, first)
                    u[level + 1, q, e, cy:] = mid
                    u[level + 1, q, e, :SUB] = jnp.where(low_lane, last, foot)
                else:
                    head = out[e - STEPS, cy - SUB :, lanes(q)].astype(F32)
                    foot = out[e - STEPS, :SUB, lanes(q)].astype(F32)
                    out[e - STEPS, cy - SUB :, lanes(q)] = jnp.where(
                        low_lane, head, first
                    ).astype(BF16)
                    out[e - STEPS, :SUB, lanes(q)] = jnp.where(
                        low_lane, last, foot
                    ).astype(BF16)

    for s in range(1, STEPS + 1):
        strips(s - 1, STEPS + s, STEPS + cx - s)

    for d in DIRS[2:6]:
        wait_recv(*d, "a")
    middle = product(STEPS, cx - STEPS)
    for q in range(groups):
        for d in DIRS[6:]:
            wait_recv(*d, q)
        for lo in (0, STEPS + cx):
            widen(q, lo, lo + STEPS)
            fringe(q, lo, lo + STEPS)
        for s in range(1, STEPS + 1):
            sweep(s - 1, q, s, STEPS + s)
            sweep(s - 1, q, STEPS + cx - s, ex - s)

    store = pltpu.make_async_copy(out, out_hbm, out_sem)
    store.start()
    total = middle + product(0, STEPS) + product(cx - STEPS, cx)
    for q in range(groups):
        ps[pl.ds(q, picks, stride=groups), :] = total[:, q * LANES : (q + 1) * LANES]

    def reduce_copy(k):
        t = lax.rem(me + k, n)
        return pltpu.make_async_remote_copy(
            src_ref=ps.at[pl.ds(pl.multiple_of(t * tile, tile), tile)],
            dst_ref=rbuf.at[k - 1], send_sem=r_send.at[k - 1], recv_sem=r_recv.at[k - 1],
            device_id=dev(t), device_id_type=MESH,
        )

    @pl.loop(1, n)
    def _(k):
        reduce_copy(k).start()

    for dx, dy in DIRS:
        @pl.when(present(dx, dy))
        def _(dx=dx, dy=dy):
            for c in copies(dx, dy):
                c.wait_send()

    @pl.loop(1, n)
    def _(k):
        reduce_copy(k).wait()

    total = ps[pl.ds(pl.multiple_of(me * tile, tile), tile), :]
    total = total + jnp.sum(rbuf[...], axis=0)
    for r in range(tile // groups):
        for q in range(groups):
            rep[r : r + 1, q * LANES : (q + 1) * LANES] = total[
                r * groups + q : r * groups + q + 1
            ]
    store.wait()


def solution(mesh):
    nx, ny = mesh.shape["gx"], mesh.shape["gy"]
    n = nx * ny

    def per_device(adjoint, conduct_x, conduct_y, pick_weights, owner_order):
        cx, cy, cols = adjoint.shape
        picks = pick_weights.shape[0]
        groups = cols // LANES
        ex, ey = cx + 2 * STEPS, cy + SUB
        tile = picks // n * groups
        vmem = pl.BlockSpec(memory_space=pltpu.VMEM)
        dma = pltpu.SemaphoreType.DMA
        any_space = pl.BlockSpec(memory_space=pl.ANY)
        smoothed, owned = pl.pallas_call(
            functools.partial(kernel, nx, ny),
            out_shape=(
                jax.ShapeDtypeStruct((cx, cy, cols), BF16),
                jax.ShapeDtypeStruct((picks // n, cols), F32),
            ),
            in_specs=[any_space] + [vmem] * 4,
            out_specs=(any_space, vmem),
            scratch_shapes=[
                pltpu.VMEM((cx, cy, cols), BF16),
                pltpu.VMEM((ex, cy, cols), BF16),
                pltpu.VMEM((2, ex, SUB, cols), BF16),
                pltpu.VMEM((len(DIRS), 2, cx, cy), F32),
                pltpu.VMEM((ex, ey, LANES), F32),
                pltpu.VMEM((ex, ey, LANES), F32),
                pltpu.VMEM((STEPS, groups, ex, ey, LANES), F32),
                pltpu.VMEM((picks * cx, LANES), F32),
                pltpu.VMEM((picks, cx * cy), BF16),
                pltpu.VMEM((picks * groups, LANES), F32),
                pltpu.VMEM((n - 1, tile, LANES), F32),
                dma,
                dma,
                dma((len(DIRS), groups)),
                dma((len(DIRS), groups)),
                dma((len(DIRS), 2)),
                dma((len(DIRS), 2)),
                dma((n - 1,)),
                dma((n - 1,)),
            ],
            compiler_params=pltpu.CompilerParams(
                collective_id=0, has_side_effects=True, vmem_limit_bytes=56 << 20
            ),
        )(adjoint, conduct_x, conduct_y, pick_weights, owner_order.reshape(1, picks))
        return smoothed, owned

    return jax.shard_map(
        per_device,
        mesh=mesh,
        in_specs=(P("gx", "gy", None), P("gx", "gy"), P("gx", "gy"), P(None, "gx", "gy"), P()),
        out_specs=(P("gx", "gy", None), P(("gx", "gy"), None)),
        check_vma=False,
    )
```
